512 devices in a mesh: dp: 64 (over z_hi, x, y), tensor: 8 (over z_lo, core).
Axes of the slice: x: 4, y: 4, z: 16 (z_hi: 4, z_lo: 4; z = z_hi * 4 + z_lo), core: 2. Of those that a mesh axis runs over, the one named last changes fastest.
Arguments:
- queries: bfloat16 [32768, 3072], P('dp', 'tensor'), may hold values from -6 to 6
- key_rows: bfloat16 [32768, 3072], P('dp', 'tensor'), may hold values from -6 to 6
- value_rows: bfloat16 [32768, 3072], P('dp', 'tensor'), may hold values from -6 to 6
- out_weight: bfloat16 [2560, 3072], P(None, 'tensor'), may hold values from -0.109375 to 0.109375
- grad_out: bfloat16 [32768, 2560], P(('dp', 'tensor')), may hold values from -48 to 48
Outputs:
- grad_query: bfloat16 [32768, 3072], P('dp', 'tensor')
- grad_keys: bfloat16 [32768, 3072], P('dp', 'tensor')
- grad_values: bfloat16 [32768, 3072], P('dp', 'tensor')
- grad_weight: float32 [2560, 3072], P('dp', 'tensor')
The draws below stay inside these ranges and needn't reach their ends.
All inputs are finite; a program needn't handle non-finite values.
Results may differ from the reference program's by a relative error of at most 0.013.
Values may be sent and summed in bfloat16 or wider, within the bound.
No kernel may reach another device: no remote copies, remote signals or barrier semaphores. Data moves between devices by JAX's collectives and lax.ppermute only.
A program may use at most 64 MiB of HBM per device.

```python
import math
import jax
import jax.numpy as jnp
from jax import lax

D = 2560
HEADS = 24
HEAD = 128
LENGTH = 256
TOKENS = 32768
N_DP = 64


def draw_pair(key):
    full_shape = (TOKENS, HEADS * HEAD)
    query_key = jax.random.fold_in(key, 11)
    rows_key = jax.random.fold_in(key, 23)
    queries = jnp.clip(jax.random.normal(query_key, full_shape, jnp.float32), -6.0, 6.0)
    key_rows = jnp.clip(jax.random.normal(rows_key, full_shape, jnp.float32), -6.0, 6.0)
    return (queries, key_rows)


def draw_queries(key, part):
    return draw_pair(key)[0].astype(jnp.bfloat16)


def draw_key_rows(key, part):
    return draw_pair(key)[1].astype(jnp.bfloat16)


def spiked(values, stream_key, source, target, parts, factor):
    owner, partner = [(jnp.arange(values.shape[axis_at]) // (values.shape[axis_at] // parts)).reshape([-1 if axis == axis_at else 1 for axis in range(values.ndim)]) for axis_at in (source, target)]
    chosen = jax.random.permutation(stream_key, parts)[partner]
    strong = (owner == chosen) | (owner == (partner + parts // 2) % parts)
    return jnp.where(strong, factor * values, values)


def levels(rng, extent, shards, smallest, high):
    def one(axis_at, parts):
        steps = jax.random.uniform(jax.random.fold_in(jax.random.fold_in(rng, 6), axis_at), (parts,), jnp.float32, smallest / len(shards), high / len(shards))
        return jnp.repeat(jnp.exp(steps), extent[axis_at] // parts).reshape((-1,) + (1,) * (len(extent) - axis_at - 1))

    level = one(*shards[0])
    for cut in shards[1:]:
        level = level * one(*cut)
    return level


def noise(stream_key, shape, deviation, most, split=(), kind=jnp.bfloat16):
    factor_of = levels(stream_key, shape, split, -0.22, 0.18) if split else 1.0
    result = jax.random.normal(stream_key, shape, jnp.float32) * deviation * factor_of
    return jnp.minimum(jnp.maximum(result, -most), most).astype(kind)


def noise_with(stream_key, shape, scale, limit, split, heavy, kind=jnp.bfloat16):
    result = scale * jax.random.normal(stream_key, shape, jnp.float32)
    if split:
        result = result * levels(stream_key, shape, split, -0.22, 0.18)
    return jnp.clip(spiked(result, jax.random.fold_in(stream_key, 3), *heavy), -limit, limit).astype(kind)


def setup_inputs(seed: int = 0) -> dict:
    key_list = jax.random.split(jax.random.key(seed), 6)
    return {
        "queries": draw_queries(jax.random.fold_in(key_list[5], 71), 0),
        "key_rows": draw_key_rows(jax.random.fold_in(key_list[5], 71), 0),
        "value_rows": noise(key_list[2], (TOKENS, HEADS * HEAD), 1.0, 6.0, ((0, 64), (1, 8))),
        "out_weight": noise(key_list[3], (D, HEADS * HEAD), (HEADS * HEAD) ** -0.5, 0.109375, ((1, 8),)),
        "grad_out": noise_with(key_list[4], (TOKENS, D), 2.0, 48.0, ((0, 512),), (0, 1, 512, 6.0)),
    }


def attention_probs(query_heads, key_heads):
    scaling = 1.0 / math.sqrt(HEAD)
    scores = jnp.einsum('qhe,khe->hqk', query_heads, key_heads) * scaling
    length = query_heads.shape[0]
    causal = lax.broadcasted_iota(jnp.int32, (length, length), 0) >= lax.broadcasted_iota(jnp.int32, (length, length), 1)
    scores = jnp.where(causal[None, :, :], scores, -jnp.inf)
    row_max = lax.optimization_barrier(jnp.max(scores, axis=-1, keepdims=True))
    exp_scores = jnp.exp(scores - row_max)
    return exp_scores / lax.optimization_barrier(jnp.sum(exp_scores, axis=-1, keepdims=True))

def reference(queries, key_rows, value_rows, out_weight, grad_out):
    head_width = HEADS * HEAD
    head_shape = (LENGTH, HEADS, HEAD)
    scaling = 1.0 / math.sqrt(HEAD)

    def one_sequence(seq_block):
        seq_queries, seq_keys, seq_values, seq_grads = seq_block
        query_heads = seq_queries.reshape(head_shape).astype(jnp.float32)
        key_heads = seq_keys.reshape(head_shape).astype(jnp.float32)
        value_heads = seq_values.reshape(head_shape).astype(jnp.float32)
        probs = attention_probs(query_heads, key_heads)
        probs_low = lax.optimization_barrier(probs.astype(jnp.bfloat16)).astype(jnp.float32)
        attended = jnp.einsum('hqk,khe->qhe', probs_low, value_heads).astype(jnp.bfloat16)
        grad_attended = jnp.dot(seq_grads, out_weight, preferred_element_type=jnp.float32).astype(jnp.bfloat16)
        grad_heads = lax.optimization_barrier(grad_attended).reshape(head_shape).astype(jnp.float32)
        grad_values = jnp.einsum('hqk,qhe->khe', probs_low, grad_heads).astype(jnp.bfloat16)
        grad_probs = jnp.einsum('qhe,khe->hqk', grad_heads, value_heads)
        row_total = lax.optimization_barrier(jnp.sum(probs * grad_probs, axis=-1, keepdims=True))
        grad_scores = (probs * (grad_probs - row_total) * scaling).astype(jnp.bfloat16)
        grad_scores = lax.optimization_barrier(grad_scores).astype(jnp.float32)
        grad_query = jnp.einsum('hqk,khe->qhe', grad_scores, key_heads).astype(jnp.bfloat16)
        grad_keys = jnp.einsum('hqk,qhe->khe', grad_scores, query_heads).astype(jnp.bfloat16)
        return (attended.reshape(LENGTH, head_width), grad_query.reshape(LENGTH, head_width), grad_keys.reshape(LENGTH, head_width), grad_values.reshape(LENGTH, head_width))
    seq_count = TOKENS // LENGTH
    blocks = (queries.reshape(seq_count, LENGTH, head_width), key_rows.reshape(seq_count, LENGTH, head_width), value_rows.reshape(seq_count, LENGTH, head_width), grad_out.reshape(seq_count, LENGTH, D))
    attended, grad_query, grad_keys, grad_values = lax.map(one_sequence, blocks)
    attended = attended.reshape(TOKENS, head_width)
    grad_weight = jnp.dot(grad_out.T, attended, preferred_element_type=jnp.float32) * (1.0 / N_DP)
    return (grad_query.reshape(TOKENS, head_width), grad_keys.reshape(TOKENS, head_width), grad_values.reshape(TOKENS, head_width), grad_weight)
```

```python
import math

import jax
import jax.numpy as jnp
import numpy as np
from jax import lax
from jax.experimental import pallas as pl
from jax.experimental.pallas import tpu as pltpu
from jax.sharding import Mesh, PartitionSpec as P

HEAD = 128
LENGTH = 256
SCALING = 1.0 / math.sqrt(HEAD)
F32 = jnp.float32
BF16 = jnp.bfloat16
AXES = ("zh", "x", "y", "zl", "core")


def dot(a, b, ca, cb):
    return lax.dot_general(a, b, (((ca,), (cb,)), ((), ())), preferred_element_type=F32)


def head_probs(q, k):
    scores = dot(q, k, 1, 1) * SCALING
    n = scores.shape[0]
    causal = lax.broadcasted_iota(jnp.int32, (n, n), 0) >= lax.broadcasted_iota(
        jnp.int32, (n, n), 1
    )
    scores = jnp.where(causal, scores, -jnp.inf)
    row_max = jnp.max(scores, axis=1, keepdims=True)
    exp_scores = jnp.exp(scores - row_max)
    return exp_scores * (1.0 / jnp.sum(exp_scores, axis=1, keepdims=True))


def tiles(shape):
    for s in range(shape[0] // LENGTH):
        for h in range(shape[1] // HEAD):
            yield pl.ds(s * LENGTH, LENGTH), pl.ds(h * HEAD, HEAD)


def attended_kernel(q_ref, k_ref, v_ref, out_ref):
    for at in tiles(out_ref.shape):
        probs = head_probs(q_ref[at], k_ref[at])
        out_ref[at] = dot(probs.astype(BF16), v_ref[at], 1, 0).astype(BF16)


def weight_kernel(rows_ref, attended_ref, out_ref):
    part = dot(rows_ref[...], attended_ref[...], 0, 0)
    out_ref[...] = part.astype(BF16).reshape(out_ref.shape)


def backward_kernel(q_ref, k_ref, v_ref, rows_ref, w_ref, gq_ref, gk_ref, gv_ref, g_ref):
    g_ref[...] = dot(rows_ref[...], w_ref[...], 1, 0).astype(BF16)
    for at in tiles(gq_ref.shape):
        q, k, v, g = q_ref[at], k_ref[at], v_ref[at], g_ref[at]
        probs = head_probs(q, k)
        gv_ref[at] = dot(probs.astype(BF16), g, 0, 0).astype(BF16)
        grad_probs = dot(g, v, 1, 1)
        row_total = jnp.sum(probs * grad_probs, axis=1, keepdims=True)
        grad_scores = (probs * (grad_probs - row_total) * SCALING).astype(BF16)
        gq_ref[at] = dot(grad_scores, k, 1, 0).astype(BF16)
        gk_ref[at] = dot(grad_scores, q, 0, 0).astype(BF16)


def call(kernel, outs, *args, scratch=()):
    return pl.pallas_call(
        kernel,
        out_shape=outs,
        scratch_shapes=scratch,
        compiler_params=pltpu.CompilerParams(vmem_limit_bytes=48 * 2**20),
        name=kernel.__name__,
    )(*args)


def gather_rows(mine):
    zl, core = lax.axis_index("zl"), lax.axis_index("core")
    far = lax.ppermute(mine, "zl", [(0, 2), (2, 0), (1, 3), (3, 1)])
    inner = lax.ppermute(mine, "zl", [(1, 2), (2, 1)])
    near = lax.ppermute(mine, "zl", [(0, 1), (1, 0), (2, 3), (3, 2)])
    outer = lax.ppermute(far, "zl", [(1, 0), (2, 3)])
    last = jnp.where((zl == 1) | (zl == 2), inner, outer)
    pieces = jnp.stack([mine, near, far, last])
    pieces = jnp.take(pieces, jnp.arange(4) ^ zl, axis=0)
    other = lax.ppermute(pieces, "core", [(0, 1), (1, 0)])
    first = jnp.where(core == 0, pieces, other)
    second = jnp.where(core == 0, other, pieces)
    return jnp.stack([first, second], axis=1).reshape(8 * mine.shape[0], mine.shape[1])


def on_device(queries, key_rows, value_rows, out_weight, grad_out):
    shape = queries.shape
    same = jax.ShapeDtypeStruct(shape, BF16)
    attended = call(attended_kernel, same, queries, key_rows, value_rows)
    rows = gather_rows(grad_out)
    d = out_weight.shape[0]
    n_dp = 64
    part = call(
        weight_kernel, jax.ShapeDtypeStruct((4, 16, d // n_dp, shape[1]), BF16), rows, attended
    )
    part = part.transpose(1, 0, 2, 3)
    got = lax.all_to_all(part, ("x", "y"), 0, 0, tiled=True)
    plane = jnp.sum(got.astype(F32), axis=0).astype(BF16)
    zh = lax.axis_index("zh")
    total = lax.dynamic_index_in_dim(plane, zh, 0, keepdims=False).astype(F32)
    for step in (2, 1, 3):
        piece = lax.dynamic_index_in_dim(plane, (zh + step) % 4, 0, keepdims=False)
        total += lax.ppermute(piece, "zh", [(i, (i + step) % 4) for i in range(4)]).astype(F32)
    grad_weight = total * (1.0 / n_dp)
    gq, gk, gv = call(
        backward_kernel,
        (same, same, same),
        queries,
        key_rows,
        value_rows,
        rows,
        out_weight,
        scratch=[pltpu.VMEM(shape, BF16)],
    )
    return gq, gk, gv, grad_weight


def solution(mesh):
    split = Mesh(np.asarray(mesh.devices).reshape(4, 4, 4, 4, 2), AXES)
    dp, tensor = ("zh", "x", "y"), ("zl", "core")
    return jax.shard_map(
        on_device,
        mesh=split,
        in_specs=(P(dp, tensor), P(dp, tensor), P(dp, tensor), P(None, tensor), P(AXES, None)),
        out_specs=(P(dp, tensor), P(dp, tensor), P(dp, tensor), P(dp, tensor)),
        check_vma=False,
    )
```

```python
import math

import jax
import jax.numpy as jnp
import numpy as np
from jax import lax
from jax.experimental import pallas as pl
from jax.experimental.pallas import tpu as pltpu
from jax.sharding import Mesh, PartitionSpec as P

HEAD = 128
LENGTH = 256
SCALING = 1.0 / math.sqrt(HEAD)
F32 = jnp.float32
BF16 = jnp.bfloat16
AXES = ("zh", "x", "y", "zl", "core")


def dot(a, b, ca, cb):
    return lax.dot_general(a, b, (((ca,), (cb,)), ((), ())), preferred_element_type=F32)


def head_probs(q, k):
    scores = dot(q, k, 1, 1) * SCALING
    n = scores.shape[0]
    causal = lax.broadcasted_iota(jnp.int32, (n, n), 0) >= lax.broadcasted_iota(
        jnp.int32, (n, n), 1
    )
    scores = jnp.where(causal, scores, -jnp.inf)
    row_max = jnp.max(scores, axis=1, keepdims=True)
    exp_scores = jnp.exp(scores - row_max)
    return exp_scores * (1.0 / jnp.sum(exp_scores, axis=1, keepdims=True))


def tiles(shape):
    for s in range(shape[0] // LENGTH):
        for h in range(shape[1] // HEAD):
            yield (pl.ds(s * LENGTH, LENGTH), pl.ds(h * HEAD, HEAD))


def attended_kernel(own_ref, q_ref, k_ref, v_ref, out_ref, kept_ref, sem):
    copy = pltpu.make_async_copy(own_ref, kept_ref, sem)
    copy.start()
    for at in tiles(out_ref.shape):
        probs = head_probs(q_ref[at], k_ref[at])
        out_ref[at] = dot(probs.astype(BF16), v_ref[at], 1, 0).astype(BF16)
    copy.wait()


def assemble(place_ref, pieces, rows_ref):
    zl, core = place_ref[0], place_ref[1]
    for at, (own, near, far, inner, outer) in ((core, pieces[:5]), (1 - core, pieces[5:])):
        rows_ref[zl, at] = own[...]
        rows_ref[zl ^ 1, at] = near[...]
        rows_ref[zl ^ 2, at] = far[...]
        rows_ref[zl ^ 3, at] = inner[...] + outer[...]
    return rows_ref[...].reshape(-1, rows_ref.shape[3])


def weight_kernel(place_ref, *refs):
    attended_ref, out_ref, kept_ref, rows_ref, sem = refs[10:]
    xy, zh, n, width = out_ref.shape
    rows = assemble(place_ref, refs[:10], rows_ref)
    keep = pltpu.make_async_copy(rows_ref, kept_ref, sem)
    keep.start()
    part = dot(rows, attended_ref[...], 0, 0).astype(BF16).reshape(zh, xy, n, width)
    for i in range(zh):
        out_ref[:, i] = part[i]
    keep.wait()


def sum_kernel(got_ref, out_ref):
    total = got_ref[0].astype(F32)
    for i in range(1, got_ref.shape[0]):
        total += got_ref[i].astype(F32)
    out_ref[...] = total.astype(out_ref.dtype)


def mean_kernel(scale, got_ref, out_ref):
    total = got_ref[0].astype(F32)
    for i in range(1, got_ref.shape[0]):
        total += got_ref[i].astype(F32)
    out_ref[...] = total * scale


def backward_kernel(rows_ref, *refs):
    ins, (gq_ref, gk_ref, gv_ref), (q_ref, k_ref, w_ref, v_ref), probs_ref, g_ref, sems = (
        refs[:4],
        refs[4:7],
        refs[7:11],
        refs[11],
        refs[12],
        refs[13],
    )
    copies = [
        pltpu.make_async_copy(a, b, sems.at[i])
        for i, (a, b) in enumerate(zip(ins, (q_ref, k_ref, w_ref, v_ref)))
    ]
    for copy in copies:
        copy.start()
    copies[0].wait()
    copies[1].wait()
    for i, at in enumerate(tiles(gq_ref.shape)):
        probs_ref[i] = head_probs(q_ref[at], k_ref[at])
    copies[2].wait()
    g_ref[...] = dot(rows_ref[...], w_ref[...], 1, 0).astype(BF16)
    copies[3].wait()
    for i, at in enumerate(tiles(gq_ref.shape)):
        q, k, v, g = q_ref[at], k_ref[at], v_ref[at], g_ref[at]
        probs = probs_ref[i]
        gv_ref[at] = dot(probs.astype(BF16), g, 0, 0).astype(BF16)
        grad_probs = dot(g, v, 1, 1)
        row_total = jnp.sum(probs * grad_probs, axis=1, keepdims=True)
        grad_scores = (probs * (grad_probs - row_total) * SCALING).astype(BF16)
        gq_ref[at] = dot(grad_scores, k, 1, 0).astype(BF16)
        gk_ref[at] = dot(grad_scores, q, 0, 0).astype(BF16)


def call(kernel, name, outs, *args, mib=48, spaces=(), out_spaces=None, scratch=()):
    vmem = pl.BlockSpec(memory_space=pltpu.VMEM)
    specs = [pl.BlockSpec(memory_space=m) for m in spaces] + [vmem] * (len(args) - len(spaces))
    many = isinstance(outs, tuple)
    return pl.pallas_call(
        kernel,
        out_shape=outs,
        in_specs=specs,
        out_specs=tuple(pl.BlockSpec(memory_space=m) for m in out_spaces or [pltpu.VMEM] * len(outs))
        if many
        else vmem,
        scratch_shapes=scratch,
        compiler_params=pltpu.CompilerParams(vmem_limit_bytes=mib * 2**20),
        name=name,
    )(*args)


def swap_cores(piece, zls=None):
    if zls is None:
        return lax.ppermute(piece, "core", [(0, 1), (1, 0)])
    pairs = [(2 * i + c, 2 * i + 1 - c) for i in zls for c in range(2)]
    return lax.ppermute(piece, ("zl", "core"), pairs)


def on_device(queries, key_rows, value_rows, out_weight, grad_out):
    shape = queries.shape
    width = shape[1]
    d = out_weight.shape[0]
    n_dp = lax.axis_size("zh") * lax.axis_size("x") * lax.axis_size("y")
    n_zh = lax.axis_size("zh")
    n_zl = lax.axis_size("zl")
    r = grad_out.shape[0]
    same = jax.ShapeDtypeStruct(shape, BF16)
    place = jnp.stack([lax.axis_index("zl"), lax.axis_index("core")]).astype(jnp.int32)

    own = grad_out
    far = lax.ppermute(own, "zl", [(0, 2), (2, 0), (1, 3), (3, 1)])
    inner = lax.ppermute(own, "zl", [(1, 2), (2, 1)])
    near = lax.ppermute(own, "zl", [(0, 1), (1, 0), (2, 3), (3, 2)])
    attended, own_kept = call(
        attended_kernel,
        "attended",
        (same, jax.ShapeDtypeStruct(own.shape, BF16)),
        pltpu.with_memory_space_constraint(own, pltpu.HBM),
        queries,
        key_rows,
        value_rows,
        spaces=[pltpu.HBM],
        scratch=[pltpu.SemaphoreType.DMA],
    )
    own_over = swap_cores(own)
    far, attended, own_over = lax.optimization_barrier((far, attended, own_over))
    outer = lax.ppermute(far, "zl", [(1, 0), (2, 3)])
    pieces = (
        own_kept,
        near,
        far,
        inner,
        outer,
        own_over,
        swap_cores(near),
        swap_cores(far),
        swap_cores(inner, (1, 2)),
        swap_cores(outer, (0, 3)),
    )
    piece_spaces = [pltpu.SMEM]
    rows_scratch = pltpu.VMEM((n_zl, 2, r, d), BF16)
    part, rows = call(
        weight_kernel,
        "weight",
        (
            jax.ShapeDtypeStruct((n_dp // n_zh, n_zh, d // n_dp, width), BF16),
            jax.ShapeDtypeStruct(rows_scratch.shape, BF16),
        ),
        place,
        *pieces,
        attended,
        spaces=piece_spaces,
        out_spaces=[pltpu.VMEM, pltpu.HBM],
        scratch=[rows_scratch, pltpu.SemaphoreType.DMA],
    )
    got = lax.all_to_all(part, ("x", "y"), 0, 0, tiled=True)
    plane = call(sum_kernel, "sum", jax.ShapeDtypeStruct(got.shape[1:], BF16), got)
    rows, plane = lax.optimization_barrier((rows, plane))
    last = lax.all_to_all(plane, "zh", 0, 0, tiled=True)
    gq, gk, gv = call(
        backward_kernel,
        "backward",
        (same, same, same),
        rows.reshape(shape[0], d),
        *(
            pltpu.with_memory_space_constraint(a, pltpu.HBM)
            for a in (queries, key_rows, out_weight, value_rows)
        ),
        spaces=[pltpu.VMEM] + [pltpu.HBM] * 4,
        scratch=[
            pltpu.VMEM(shape, BF16),
            pltpu.VMEM(shape, BF16),
            pltpu.VMEM(out_weight.shape, BF16),
            pltpu.VMEM(shape, BF16),
            pltpu.VMEM((shape[0] // LENGTH * width // HEAD, LENGTH, LENGTH), F32),
            pltpu.VMEM(shape, BF16),
            pltpu.SemaphoreType.DMA((4,)),
        ],
    )
    grad_weight = call(
        lambda a, b: mean_kernel(1.0 / n_dp, a, b),
        "mean",
        jax.ShapeDtypeStruct(last.shape[1:], F32),
        last,
    )
    return gq, gk, gv, grad_weight


def solution(mesh):
    split = Mesh(np.asarray(mesh.devices).reshape(4, 4, 4, 4, 2), AXES)
    dp, tensor = ("zh", "x", "y"), ("zl", "core")
    return jax.shard_map(
        on_device,
        mesh=split,
        in_specs=(P(dp, tensor), P(dp, tensor), P(dp, tensor), P(None, tensor), P(AXES, None)),
        out_specs=(P(dp, tensor), P(dp, tensor), P(dp, tensor), P(dp, tensor)),
        check_vma=False,
    )
```

```python
import math

import jax
import jax.numpy as jnp
import numpy as np
from jax import lax
from jax.experimental import pallas as pl
from jax.experimental.pallas import tpu as pltpu
from jax.sharding import Mesh, PartitionSpec as P

HEAD = 128
LENGTH = 256
SCALING = 1.0 / math.sqrt(HEAD)
F32 = jnp.float32
BF16 = jnp.bfloat16
AXES = ("zh", "x", "y", "zl", "core")


def dot(a, b, ca, cb):
    return lax.dot_general(a, b, (((ca,), (cb,)), ((), ())), preferred_element_type=F32)


ORDER_ZH = [2, 3, 0, 1]
ORDER_XY = [10, 11, 8, 9, 14, 15, 12, 13, 2, 3, 0, 1, 6, 7, 4, 5]
HALVES = ((0, LENGTH // 2), (LENGTH // 2, LENGTH))


def half_probs(q, k, at, end):
    scores = dot(q[at:end], k[:end], 1, 1) * SCALING
    causal = at + lax.broadcasted_iota(jnp.int32, scores.shape, 0) >= lax.broadcasted_iota(
        jnp.int32, scores.shape, 1
    )
    scores = jnp.where(causal, scores, -jnp.inf)
    row_max = jnp.max(scores, axis=1, keepdims=True)
    exp_scores = jnp.exp(scores - row_max)
    return exp_scores * (1.0 / jnp.sum(exp_scores, axis=1, keepdims=True))


def widened(first, second):
    none = jnp.zeros((first.shape[0], second.shape[1] - first.shape[1]), first.dtype)
    return jnp.concatenate([jnp.concatenate([first, none], axis=1), second], axis=0)


def tiles(shape):
    for s in range(shape[0] // LENGTH):
        for h in range(shape[1] // HEAD):
            yield (pl.ds(s * LENGTH, LENGTH), pl.ds(h * HEAD, HEAD))


def fetch(sources, targets, sems):
    copies = [pltpu.make_async_copy(a, b, sems.at[i]) for i, (a, b) in enumerate(zip(sources, targets))]
    for copy in copies:
        copy.start()
    return copies


def attended_kernel(*refs):
    ins, (out_ref, own_ref, q_ref, k_ref, v_ref, sems) = refs[:4], refs[4:]
    for copy in fetch(ins, (q_ref, k_ref, v_ref, own_ref), sems):
        copy.wait()
    for at in tiles(out_ref.shape):
        q, k = q_ref[at], k_ref[at]
        probs = widened(*(half_probs(q, k, *half).astype(BF16) for half in HALVES))
        out_ref[at] = dot(probs, v_ref[at], 1, 0).astype(BF16)


def assemble(place_ref, pieces, rows_ref):
    zl, core = place_ref[0], place_ref[1]
    for at, (own, near, far, inner, outer) in ((core, pieces[:5]), (1 - core, pieces[5:])):
        rows_ref[zl, at] = own[...]
        rows_ref[zl ^ 1, at] = near[...]
        rows_ref[zl ^ 2, at] = far[...]
        rows_ref[zl ^ 3, at] = inner[...] + outer[...]
    return rows_ref[...].reshape(-1, rows_ref.shape[3])


def weight_kernel(place_ref, *refs):
    attended_ref, out_ref, kept_ref, rows_ref, sem = refs[10:]
    xy, zh, n, width = out_ref.shape
    rows = assemble(place_ref, refs[:10], rows_ref)
    keep = pltpu.make_async_copy(rows_ref, kept_ref, sem)
    keep.start()
    part = dot(rows, attended_ref[...], 0, 0).astype(BF16).reshape(zh, xy, n, width)
    for i in range(zh):
        for j, block in enumerate(ORDER_XY):
            out_ref[j, i] = part[i, block]
    keep.wait()


def sum_kernel(got_ref, out_ref):
    total = got_ref[0].astype(F32)
    for i in range(1, got_ref.shape[0]):
        total += got_ref[i].astype(F32)
    for i, block in enumerate(ORDER_ZH):
        out_ref[i] = total[block].astype(out_ref.dtype)


def mean_kernel(scale, got_ref, out_ref):
    total = got_ref[0].astype(F32)
    for i in range(1, got_ref.shape[0]):
        total += got_ref[i].astype(F32)
    out_ref[...] = total * scale


def backward_kernel(rows_ref, *refs):
    ins, (gq_ref, gk_ref, gv_ref) = refs[:4], refs[4:7]
    q_ref, k_ref, w_ref, v_ref, first_ref, second_ref, g_ref, sems = refs[7:]
    copies = fetch(ins, (q_ref, k_ref, w_ref, v_ref), sems)
    copies[0].wait()
    copies[1].wait()
    for i, at in enumerate(tiles(gq_ref.shape)):
        q, k = q_ref[at], k_ref[at]
        for ref, half in zip((first_ref, second_ref), HALVES):
            ref[i] = half_probs(q, k, *half)
    copies[2].wait()
    g_ref[...] = dot(rows_ref[...], w_ref[...], 1, 0).astype(BF16)
    copies[3].wait()
    for i, at in enumerate(tiles(gq_ref.shape)):
        q, k, v, g = q_ref[at], k_ref[at], v_ref[at], g_ref[at]
        probs_low, grad_scores = [], []
        for ref, (start, end) in zip((first_ref, second_ref), HALVES):
            probs = ref[i]
            grad_probs = dot(g[start:end], v[:end], 1, 1)
            row_total = jnp.sum(probs * grad_probs, axis=1, keepdims=True)
            probs_low.append(probs.astype(BF16))
            grad_scores.append((probs * (grad_probs - row_total) * SCALING).astype(BF16))
        probs_low, grad_scores = widened(*probs_low), widened(*grad_scores)
        gv_ref[at] = dot(probs_low, g, 0, 0).astype(BF16)
        gq_ref[at] = dot(grad_scores, k, 1, 0).astype(BF16)
        gk_ref[at] = dot(grad_scores, q, 0, 0).astype(BF16)


def call(kernel, name, outs, *args, mib=48, spaces=(), out_spaces=None, scratch=()):
    vmem = pl.BlockSpec(memory_space=pltpu.VMEM)
    specs = [pl.BlockSpec(memory_space=m) for m in spaces] + [vmem] * (len(args) - len(spaces))
    many = isinstance(outs, tuple)
    return pl.pallas_call(
        kernel,
        out_shape=outs,
        in_specs=specs,
        out_specs=tuple(pl.BlockSpec(memory_space=m) for m in out_spaces or [pltpu.VMEM] * len(outs))
        if many
        else vmem,
        scratch_shapes=scratch,
        compiler_params=pltpu.CompilerParams(vmem_limit_bytes=mib * 2**20),
        name=name,
    )(*args)


def swap_cores(piece, zls=None):
    if zls is None:
        return lax.ppermute(piece, "core", [(0, 1), (1, 0)])
    pairs = [(2 * i + c, 2 * i + 1 - c) for i in zls for c in range(2)]
    return lax.ppermute(piece, ("zl", "core"), pairs)


def on_device(queries, key_rows, value_rows, out_weight, grad_out):
    shape = queries.shape
    width = shape[1]
    d = out_weight.shape[0]
    n_dp = lax.axis_size("zh") * lax.axis_size("x") * lax.axis_size("y")
    n_zh = lax.axis_size("zh")
    n_zl = lax.axis_size("zl")
    r = grad_out.shape[0]
    same = jax.ShapeDtypeStruct(shape, BF16)
    place = jnp.stack([lax.axis_index("zl"), lax.axis_index("core")]).astype(jnp.int32)

    own = grad_out
    far = lax.ppermute(own, "zl", [(0, 2), (2, 0), (1, 3), (3, 1)])
    inner = lax.ppermute(own, "zl", [(1, 2), (2, 1)])
    near = lax.ppermute(own, "zl", [(0, 1), (1, 0), (2, 3), (3, 2)])
    n_tiles = shape[0] // LENGTH * width // HEAD
    attended, own_kept = call(
        attended_kernel,
        "attended",
        (same, jax.ShapeDtypeStruct(own.shape, BF16)),
        *(
            pltpu.with_memory_space_constraint(a, pltpu.HBM)
            for a in (queries, key_rows, value_rows, own)
        ),
        spaces=[pltpu.HBM] * 4,
        scratch=[pltpu.VMEM(shape, BF16)] * 3 + [pltpu.SemaphoreType.DMA((4,))],
    )
    own_over = swap_cores(own)
    far, attended, own_over = lax.optimization_barrier((far, attended, own_over))
    outer = lax.ppermute(far, "zl", [(1, 0), (2, 3)])
    pieces = (
        own_kept,
        near,
        far,
        inner,
        outer,
        own_over,
        swap_cores(near),
        swap_cores(far),
        swap_cores(inner, (1, 2)),
        swap_cores(outer, (0, 3)),
    )
    piece_spaces = [pltpu.SMEM]
    rows_scratch = pltpu.VMEM((n_zl, 2, r, d), BF16)
    part, rows = call(
        weight_kernel,
        "weight",
        (
            jax.ShapeDtypeStruct((n_dp // n_zh, n_zh, d // n_dp, width), BF16),
            jax.ShapeDtypeStruct(rows_scratch.shape, BF16),
        ),
        place,
        *pieces,
        attended,
        spaces=piece_spaces,
        out_spaces=[pltpu.VMEM, pltpu.HBM],
        scratch=[rows_scratch, pltpu.SemaphoreType.DMA],
    )
    got = lax.all_to_all(part, ("x", "y"), 0, 0, axis_index_groups=[ORDER_XY], tiled=True)
    plane = call(sum_kernel, "sum", jax.ShapeDtypeStruct(got.shape[1:], BF16), got)
    rows, plane = lax.optimization_barrier((rows, plane))
    last = lax.all_to_all(plane, "zh", 0, 0, axis_index_groups=[ORDER_ZH], tiled=True)
    gq, gk, gv = call(
        backward_kernel,
        "backward",
        (same, same, same),
        rows.reshape(shape[0], d),
        *(
            pltpu.with_memory_space_constraint(a, pltpu.HBM)
            for a in (queries, key_rows, out_weight, value_rows)
        ),
        spaces=[pltpu.VMEM] + [pltpu.HBM] * 4,
        scratch=[
            pltpu.VMEM(shape, BF16),
            pltpu.VMEM(shape, BF16),
            pltpu.VMEM(out_weight.shape, BF16),
            pltpu.VMEM(shape, BF16),
            *(pltpu.VMEM((n_tiles, end - at, end), F32) for at, end in HALVES),
            pltpu.VMEM(shape, BF16),
            pltpu.SemaphoreType.DMA((4,)),
        ],
    )
    grad_weight = call(
        lambda a, b: mean_kernel(1.0 / n_dp, a, b),
        "mean",
        jax.ShapeDtypeStruct(last.shape[1:], F32),
        last,
    )
    return gq, gk, gv, grad_weight


def solution(mesh):
    split = Mesh(np.asarray(mesh.devices).reshape(4, 4, 4, 4, 2), AXES)
    dp, tensor = ("zh", "x", "y"), ("zl", "core")
    return jax.shard_map(
        on_device,
        mesh=split,
        in_specs=(P(dp, tensor), P(dp, tensor), P(dp, tensor), P(None, tensor), P(AXES, None)),
        out_specs=(P(dp, tensor), P(dp, tensor), P(dp, tensor), P(dp, tensor)),
        check_vma=False,
    )
```

```python
import math

import jax
import jax.numpy as jnp
import numpy as np
from jax import lax
from jax.experimental import pallas as pl
from jax.experimental.pallas import tpu as pltpu
from jax.sharding import Mesh, PartitionSpec as P

HEAD = 128
LENGTH = 256
SCALING = 1.0 / math.sqrt(HEAD)
F32 = jnp.float32
BF16 = jnp.bfloat16
AXES = ("zh", "x", "y", "zl", "core")


def dot(a, b, ca, cb):
    return lax.dot_general(a, b, (((ca,), (cb,)), ((), ())), preferred_element_type=F32)


ORDER_ZH = [2, 3, 0, 1]
ORDER_XY = [10, 11, 8, 9, 14, 15, 12, 13, 2, 3, 0, 1, 6, 7, 4, 5]
HALVES = ((0, LENGTH // 2), (LENGTH // 2, LENGTH))


def half_probs(q, k, at, end):
    scores = dot(q[at:end], k[:end], 1, 1) * SCALING
    causal = at + lax.broadcasted_iota(jnp.int32, scores.shape, 0) >= lax.broadcasted_iota(
        jnp.int32, scores.shape, 1
    )
    scores = jnp.where(causal, scores, -jnp.inf)
    row_max = jnp.max(scores, axis=1, keepdims=True)
    exp_scores = jnp.exp(scores - row_max)
    return exp_scores * (1.0 / jnp.sum(exp_scores, axis=1, keepdims=True))


def widened(first, second):
    none = jnp.zeros((first.shape[0], second.shape[1] - first.shape[1]), first.dtype)
    return jnp.concatenate([jnp.concatenate([first, none], axis=1), second], axis=0)


def tiles(shape):
    for s in range(shape[0] // LENGTH):
        for h in range(shape[1] // HEAD):
            yield (pl.ds(s * LENGTH, LENGTH), pl.ds(h * HEAD, HEAD))


def fetch(sources, targets, sems):
    copies = [pltpu.make_async_copy(a, b, sems.at[i]) for i, (a, b) in enumerate(zip(sources, targets))]
    for copy in copies:
        copy.start()
    return copies


def attended_kernel(*refs):
    ins, (out_ref, own_ref, q_ref, k_ref, v_ref, sems) = refs[:4], refs[4:]
    for copy in fetch(ins, (q_ref, k_ref, v_ref, own_ref), sems):
        copy.wait()
    for at in tiles(out_ref.shape):
        q, k = q_ref[at], k_ref[at]
        probs = widened(*(half_probs(q, k, *half).astype(BF16) for half in HALVES))
        out_ref[at] = dot(probs, v_ref[at], 1, 0).astype(BF16)


def assemble(place_ref, pieces, rows_ref):
    zl, core = place_ref[0], place_ref[1]
    for at, (own, near, far, inner, outer) in ((core, pieces[:5]), (1 - core, pieces[5:])):
        rows_ref[zl, at] = own[...]
        rows_ref[zl ^ 1, at] = near[...]
        rows_ref[zl ^ 2, at] = far[...]
        rows_ref[zl ^ 3, at] = inner[...] + outer[...]
    return rows_ref[...].reshape(-1, rows_ref.shape[3])


def weight_kernel(place_ref, *refs):
    attended_ref, out_ref, kept_ref, rows_ref, sem = refs[10:]
    xy, zh, n, width = out_ref.shape
    rows = assemble(place_ref, refs[:10], rows_ref)
    keep = pltpu.make_async_copy(rows_ref, kept_ref, sem)
    keep.start()
    part = dot(rows, attended_ref[...], 0, 0).astype(BF16).reshape(zh, xy, n, width)
    for i in range(zh):
        for j, block in enumerate(ORDER_XY):
            out_ref[j, i] = part[i, block]
    keep.wait()


def sum_kernel(got_ref, out_ref):
    total = got_ref[0].astype(F32)
    for i in range(1, got_ref.shape[0]):
        total += got_ref[i].astype(F32)
    for i, block in enumerate(ORDER_ZH):
        out_ref[i] = total[block].astype(out_ref.dtype)


def mean_kernel(scale, got_ref, out_ref):
    total = got_ref[0].astype(F32)
    for i in range(1, got_ref.shape[0]):
        total += got_ref[i].astype(F32)
    out_ref[...] = total * scale


def backward_kernel(rows_ref, q_ref, k_ref, *refs):
    ins, (gq_ref, gk_ref, gv_ref) = refs[:2], refs[2:5]
    w_ref, v_ref, first_ref, second_ref, g_ref, sems = refs[5:]
    copies = fetch(ins, (w_ref, v_ref), sems)
    for i, at in enumerate(tiles(gq_ref.shape)):
        q, k = q_ref[at], k_ref[at]
        for ref, half in zip((first_ref, second_ref), HALVES):
            ref[i] = half_probs(q, k, *half)
    copies[0].wait()
    g_ref[...] = dot(rows_ref[...], w_ref[...], 1, 0).astype(BF16)
    copies[1].wait()
    saved = []
    for i, at in enumerate(tiles(gq_ref.shape)):
        v, g = v_ref[at], g_ref[at]
        probs_low, grad_scores = [], []
        for ref, (start, end) in zip((first_ref, second_ref), HALVES):
            probs = ref[i]
            grad_probs = dot(g[start:end], v[:end], 1, 1)
            row_total = jnp.sum(probs * grad_probs, axis=1, keepdims=True)
            probs_low.append(probs.astype(BF16))
            grad_scores.append((probs * (grad_probs - row_total) * SCALING).astype(BF16))
        saved.append((widened(*probs_low), widened(*grad_scores)))
    for (probs_low, grad_scores), at in zip(saved, tiles(gq_ref.shape)):
        gv_ref[at] = dot(probs_low, g_ref[at], 0, 0).astype(BF16)
        gq_ref[at] = dot(grad_scores, k_ref[at], 1, 0).astype(BF16)
        gk_ref[at] = dot(grad_scores, q_ref[at], 0, 0).astype(BF16)


def call(kernel, name, outs, *args, mib=48, spaces=(), out_spaces=None, scratch=()):
    vmem = pl.BlockSpec(memory_space=pltpu.VMEM)
    specs = [pl.BlockSpec(memory_space=m) for m in spaces] + [vmem] * (len(args) - len(spaces))
    many = isinstance(outs, tuple)
    return pl.pallas_call(
        kernel,
        out_shape=outs,
        in_specs=specs,
        out_specs=tuple(pl.BlockSpec(memory_space=m) for m in out_spaces or [pltpu.VMEM] * len(outs))
        if many
        else vmem,
        scratch_shapes=scratch,
        compiler_params=pltpu.CompilerParams(vmem_limit_bytes=mib * 2**20),
        name=name,
    )(*args)


def swap_cores(piece, zls=None):
    if zls is None:
        return lax.ppermute(piece, "core", [(0, 1), (1, 0)])
    pairs = [(2 * i + c, 2 * i + 1 - c) for i in zls for c in range(2)]
    return lax.ppermute(piece, ("zl", "core"), pairs)


def on_device(queries, key_rows, value_rows, out_weight, grad_out):
    shape = queries.shape
    width = shape[1]
    d = out_weight.shape[0]
    n_dp = lax.axis_size("zh") * lax.axis_size("x") * lax.axis_size("y")
    n_zh = lax.axis_size("zh")
    n_zl = lax.axis_size("zl")
    r = grad_out.shape[0]
    same = jax.ShapeDtypeStruct(shape, BF16)
    place = jnp.stack([lax.axis_index("zl"), lax.axis_index("core")]).astype(jnp.int32)

    own = grad_out
    far = lax.ppermute(own, "zl", [(0, 2), (2, 0), (1, 3), (3, 1)])
    inner = lax.ppermute(own, "zl", [(1, 2), (2, 1)])
    near = lax.ppermute(own, "zl", [(0, 1), (1, 0), (2, 3), (3, 2)])
    n_tiles = shape[0] // LENGTH * width // HEAD
    attended, own_kept = call(
        attended_kernel,
        "attended",
        (same, jax.ShapeDtypeStruct(own.shape, BF16)),
        *(
            pltpu.with_memory_space_constraint(a, pltpu.HBM)
            for a in (queries, key_rows, value_rows, own)
        ),
        spaces=[pltpu.HBM] * 4,
        scratch=[pltpu.VMEM(shape, BF16)] * 3 + [pltpu.SemaphoreType.DMA((4,))],
    )
    own_over = swap_cores(own)
    far, attended, own_over = lax.optimization_barrier((far, attended, own_over))
    outer = lax.ppermute(far, "zl", [(1, 0), (2, 3)])
    pieces = (
        own_kept,
        near,
        far,
        inner,
        outer,
        own_over,
        swap_cores(near),
        swap_cores(far),
        swap_cores(inner, (1, 2)),
        swap_cores(outer, (0, 3)),
    )
    piece_spaces = [pltpu.SMEM]
    rows_scratch = pltpu.VMEM((n_zl, 2, r, d), BF16)
    part, rows = call(
        weight_kernel,
        "weight",
        (
            jax.ShapeDtypeStruct((n_dp // n_zh, n_zh, d // n_dp, width), BF16),
            jax.ShapeDtypeStruct(rows_scratch.shape, BF16),
        ),
        place,
        *pieces,
        attended,
        spaces=piece_spaces,
        out_spaces=[pltpu.VMEM, pltpu.HBM],
        scratch=[rows_scratch, pltpu.SemaphoreType.DMA],
    )
    got = lax.all_to_all(part, ("x", "y"), 0, 0, axis_index_groups=[ORDER_XY], tiled=True)
    plane = call(sum_kernel, "sum", jax.ShapeDtypeStruct(got.shape[1:], BF16), got)
    rows, plane = lax.optimization_barrier((rows, plane))
    last = lax.all_to_all(plane, "zh", 0, 0, axis_index_groups=[ORDER_ZH], tiled=True)
    gq, gk, gv = call(
        backward_kernel,
        "backward",
        (same, same, same),
        rows.reshape(shape[0], d),
        queries,
        key_rows,
        *(pltpu.with_memory_space_constraint(a, pltpu.HBM) for a in (out_weight, value_rows)),
        spaces=[pltpu.VMEM] * 3 + [pltpu.HBM] * 2,
        scratch=[
            pltpu.VMEM(out_weight.shape, BF16),
            pltpu.VMEM(shape, BF16),
            *(pltpu.VMEM((n_tiles, end - at, end), F32) for at, end in HALVES),
            pltpu.VMEM(shape, BF16),
            pltpu.SemaphoreType.DMA((2,)),
        ],
    )
    grad_weight = call(
        lambda a, b: mean_kernel(1.0 / n_dp, a, b),
        "mean",
        jax.ShapeDtypeStruct(last.shape[1:], F32),
        last,
    )
    return gq, gk, gv, grad_weight


def solution(mesh):
    split = Mesh(np.asarray(mesh.devices).reshape(4, 4, 4, 4, 2), AXES)
    dp, tensor = ("zh", "x", "y"), ("zl", "core")
    return jax.shard_map(
        on_device,
        mesh=split,
        in_specs=(P(dp, tensor), P(dp, tensor), P(dp, tensor), P(None, tensor), P(AXES, None)),
        out_specs=(P(dp, tensor), P(dp, tensor), P(dp, tensor), P(dp, tensor)),
        check_vma=False,
    )
```
